512 devices in a mesh: pair: 16 (over x, y_hi, core), virt: 32 (over z, y_lo).
Axes of the slice: x: 4, y: 8 (y_hi: 2, y_lo: 4; y = y_hi * 4 + y_lo), z: 8, core: 2. Of those that a mesh axis runs over, the one named last changes fastest.
Arguments:
- amplitudes: bfloat16 [16384, 1024], P(('pair', 'virt')), may hold values from -6 to 6
- integrals: bfloat16 [1024, 65536], P('pair', 'virt'), may hold values from -0.1875 to 0.1875
- amp_mask: int32 [256, 16], P('pair'), may hold values from 0 to 1, as said below
- integral_mask: int32 [16, 1024], P('pair', 'virt'), may hold values 0 or 1
Outputs:
- ladder: bfloat16 [16384, 65536], P('pair', 'virt')
The draws below stay inside these ranges and needn't reach their ends.
Inputs may be any that keep to these rules, and one draw needn't show every extreme that they name: `amp_mask`: 0 or 1. For every block of 16 consecutive ij tiles, the cd tiles that hold nonzeros lie within one cyclic window of cd tiles common to the block, whose length may differ from block to block.
All inputs are finite; a program needn't handle non-finite values. No bound on the sum of `integral_mask` on one device may be relied on, other than what follows from the above.
Results may differ from the reference program's by a relative error of at most 0.001.
Values may be sent and summed in bfloat16 or wider, within the bound.
No kernel may reach another device: no remote copies, remote signals or barrier semaphores. Data moves between devices by JAX's collectives and lax.ppermute only.
A program may use at most 64 MiB of HBM per device.

```python
import jax
import jax.numpy as jnp
from jax import lax

TILE = 64
IJ_DEV = 1024
NIJ = 16384
NCD = 1024
NAB = 65536


def draw_amp_mask(key, part):
    tile_rows = NIJ // TILE
    tile_columns = NCD // TILE
    per_block = IJ_DEV // TILE
    block_count = tile_rows // per_block
    centre_key = jax.random.fold_in(key, 11)
    width_key = jax.random.fold_in(key, 23)
    keep_key = jax.random.fold_in(key, 37)
    centre = jax.random.randint(centre_key, (block_count,), 0, tile_columns)
    widths = jax.random.randint(width_key, (block_count,), max(1, tile_columns // 4), tile_columns + 1)
    keeper = jax.random.randint(keep_key, (tile_rows, tile_columns), 0, 4) > 0
    block_of = jnp.arange(tile_rows) // per_block
    distance = (jnp.arange(tile_columns)[None, :] - centre[block_of][:, None]) % tile_columns
    inside = distance < widths[block_of][:, None]
    return (inside & keeper).astype(jnp.int32)


def plant(values, own_key, smallest, largest):
    index_at = [jax.random.randint(jax.random.fold_in(own_key, axis), (), 0, length) for axis, length in enumerate(values.shape)]
    longest = values.shape.index(max(values.shape))
    beside = index_at[:longest] + [(index_at[longest] + 1) % values.shape[longest]] + index_at[longest + 1:]
    return values.at[tuple(index_at)].set(smallest).at[tuple(beside)].set(largest)


def block_scale(rng, extent, cuts, least, high):
    gain, own = 1.0, jax.random.fold_in(rng, 6)
    for axis_at, blocks in cuts:
        draws = jnp.exp(jax.random.uniform(jax.random.fold_in(own, axis_at), (blocks,), jnp.float32, least / len(cuts), high / len(cuts)))
        gain = gain * jnp.repeat(draws, extent[axis_at] // blocks).reshape([-1 if axis == axis_at else 1 for axis in range(len(extent))])
    return gain


def bell_draw(stream_key, dims, spread, limit, shards=(), held_as=jnp.bfloat16):
    gain = block_scale(stream_key, dims, shards, -0.22, 0.18) if shards else 1.0
    values = jax.random.normal(stream_key, dims, jnp.float32) * spread * gain
    return jnp.minimum(jnp.maximum(values, -limit), limit).astype(held_as)


def setup_inputs(seed: int = 0) -> dict:
    key_of = jax.random.split(jax.random.key(seed), 5)
    amplitudes = bell_draw(key_of[0], (NIJ, NCD), 1.0, 6.0, ((0, 512),))
    integrals = bell_draw(key_of[1], (NCD, NAB), NCD ** -0.5, 0.1875, ((0, 16), (1, 32)))
    amp_mask = draw_amp_mask(jax.random.fold_in(key_of[4], 71), 0)
    integral_mask = plant((jax.random.randint(key_of[3], (NCD // TILE, NAB // TILE), 0, 4) < 3).astype(jnp.int32), jax.random.fold_in(key_of[3], 1), 0, 1)
    return dict(amplitudes=amplitudes, integrals=integrals, amp_mask=amp_mask, integral_mask=integral_mask)


def widened_mask(values, mask):
    tile_rows, tile_columns = mask.shape
    shaped = values.reshape(tile_rows, TILE, tile_columns, TILE)
    return (shaped * mask.astype(values.dtype)[:, None, :, None]).reshape(values.shape)


def reference(amplitudes, integrals, amp_mask, integral_mask):
    tmask = widened_mask(amplitudes, amp_mask)
    virtual_mask = widened_mask(integrals, integral_mask)
    blocks = tmask.reshape(NIJ // IJ_DEV, IJ_DEV, NCD)

    def one_block(block_row_list):
        return jnp.dot(block_row_list, virtual_mask, preferred_element_type=jnp.float32).astype(jnp.bfloat16)

    result = lax.map(one_block, blocks)
    return result.reshape(NIJ, NAB)
```

```python
import functools

import jax
import jax.numpy as jnp
from jax import lax
from jax.experimental import pallas as pl
from jax.experimental.pallas import tpu as pltpu
from jax.sharding import Mesh, PartitionSpec as P

TILE = 64
AXES = ("x", "yh", "c", "zh", "zl", "yl")


def masked_amp(amplitudes, amp_mask):
    tile_row = (lax.axis_index("zh") * 16 + lax.axis_index("zl") * 4 + lax.axis_index("yl")) // 2
    row = lax.dynamic_slice_in_dim(amp_mask, tile_row, 1, 0).astype(amplitudes.dtype)
    wide = jnp.broadcast_to(row[:, :, None], (1, 16, TILE)).reshape(1, 1024)
    return amplitudes * wide


def masked_int(integrals, integral_mask):
    row = integral_mask.astype(integrals.dtype)
    wide = jnp.broadcast_to(row[:, :, None], (1, 32, TILE)).reshape(1, 2048)
    return integrals * wide


def shift_z(value, by):
    pairs = [(z, (z + by) % 8) for z in range(8)]
    return lax.ppermute(value, ("zh", "zl"), pairs)


def shift(value, axis, size, by):
    return lax.ppermute(value, axis, [(i, (i + by) % size) for i in range(size)])


def matmul_kernel(pos, *refs):
    a_refs, b_refs, out_ref, b_all, sems = refs[:4], refs[4:12], refs[12], refs[13], refs[14]
    step = pl.program_id(0)
    x, yh, c = pos[1], pos[2], pos[3]

    @pl.when(step == 0)
    def _():
        copies = []
        for side in range(2):
            for hop in range(4):
                for tile in range(2):
                    owner_x = lax.rem(x + hop, 4)
                    owner_y = lax.rem(yh + tile, 2)
                    owner_c = lax.rem(c + side, 2)
                    at = pl.multiple_of(owner_x * 256 + owner_y * 128 + owner_c * 64, 64)
                    n = side * 4 + hop
                    copies.append(pltpu.make_async_copy(
                        b_refs[n].at[pl.ds(tile * TILE, TILE), :],
                        b_all.at[pl.ds(at, TILE), :],
                        sems.at[n * 2 + tile],
                    ))
        for copy in copies:
            copy.start()
        for copy in copies:
            copy.wait()

    for piece in range(4):
        @pl.when(step // 2 == piece)
        def _():
            out_ref[...] = jnp.dot(
                a_refs[piece][...], b_all[...], preferred_element_type=jnp.float32
            ).astype(out_ref.dtype)


def matmul(pos, a_pieces, b_pieces):
    def a_map(piece):
        return lambda s, pos: (jnp.clip(s - 2 * piece, 0, 1), 0)

    def out_map(s, pos):
        return (lax.rem(s, 2) * 4 + lax.rem(pos[0] + s // 2, 4), 0)

    grid_spec = pltpu.PrefetchScalarGridSpec(
        num_scalar_prefetch=1,
        grid=(8,),
        in_specs=[pl.BlockSpec((128, 1024), a_map(k)) for k in range(4)]
        + [pl.BlockSpec(memory_space=pl.ANY)] * 8,
        out_specs=pl.BlockSpec((128, 2048), out_map),
        scratch_shapes=[pltpu.VMEM((1024, 2048), jnp.bfloat16), pltpu.SemaphoreType.DMA((16,))],
    )
    return pl.pallas_call(
        matmul_kernel,
        grid_spec=grid_spec,
        out_shape=jax.ShapeDtypeStruct((1024, 2048), jnp.bfloat16),
        name="ladder_matmul",
    )(pos, *a_pieces, *b_pieces)


def on_device(amplitudes, integrals, amp_mask, integral_mask):
    own_b = masked_int(integrals, integral_mask)
    far_b = shift(own_b, "yh", 2, 1)
    own_a = masked_amp(amplitudes, amp_mask)
    fan = jnp.broadcast_to(own_a[None], (8, 32, 1024))
    a0 = lax.all_to_all(fan, ("zh", "yl"), 0, 0).reshape(256, 1024)
    b0 = jnp.concatenate([own_b, far_b])
    b_here = [b0, shift(b0, "x", 4, -1), shift(b0, "x", 4, 2), shift(b0, "x", 4, 1)]
    a_here = [a0, shift_z(a0, -1), shift_z(a0, 2), shift_z(a0, 1)]
    b_there = [shift(b, "c", 2, 1) for b in b_here]
    pos = jnp.stack([lax.axis_index(a) for a in ("zl", "x", "yh", "c")]).astype(jnp.int32)
    return matmul(pos, a_here, b_here + b_there)


def solution(mesh):
    fine = Mesh(mesh.devices.reshape(4, 2, 2, 2, 4, 4), AXES)
    pair, virt = AXES[:3], AXES[3:]
    in_specs = (P(AXES, None), P(pair, virt), P(pair, None), P(pair, virt))
    return jax.shard_map(on_device, mesh=fine, in_specs=in_specs, out_specs=P(pair, virt), check_vma=False)
```

```python
import jax
import jax.numpy as jnp
from jax import lax
from jax.experimental import pallas as pl
from jax.experimental.pallas import tpu as pltpu
from jax.sharding import Mesh, PartitionSpec as P


TILE = 64
AXES = ("x", "yh", "c", "zh", "zl", "yl")


def prep_kernel(pos, am_ref, im_ref, a_ref, b_ref, own_a_ref, own_b_ref):
    tile_row = pos[0] // 8
    lane = lax.broadcasted_iota(jnp.int32, (8, 128), 1)

    def spread(low, high):
        both = jnp.where(lane < TILE, low, high)[:1]
        return both.astype(jnp.float32).astype(jnp.bfloat16)

    for g in range(16):
        span = pl.ds(g * 128, 128)
        own_b_ref[:, span] = b_ref[:, span] * spread(im_ref[0, 2 * g], im_ref[0, 2 * g + 1])
    for g in range(8):
        span = pl.ds(g * 128, 128)
        own_a_ref[:, span] = a_ref[:, span] * spread(am_ref[tile_row, 2 * g], am_ref[tile_row, 2 * g + 1])


def prep(pos, amp_mask, integral_mask, amplitudes, integrals):
    smem, vmem = pl.BlockSpec(memory_space=pltpu.SMEM), pl.BlockSpec(memory_space=pltpu.VMEM)
    shapes = ((32, 1024), (64, 2048))
    return pl.pallas_call(
        prep_kernel,
        in_specs=[smem, smem, smem, vmem, vmem],
        out_specs=[vmem] * 2,
        out_shape=[jax.ShapeDtypeStruct(s, jnp.bfloat16) for s in shapes],
        name="prep",
    )(pos, amp_mask, integral_mask, amplitudes, integrals)


def shift_z(value, by):
    return lax.ppermute(value, ("zh", "zl"), [(z, (z + by) % 8) for z in range(8)])


def shift(value, axis, size, by):
    return lax.ppermute(value, axis, [(i, (i + by) % size) for i in range(size)])


def swap_y(value, by):
    return lax.ppermute(value, "yl", [(y, y ^ by) for y in range(4)])


def all_x(fan):
    return lax.all_to_all(fan, "x", 0, 0)


def matmul_kernel(hops, pos, *refs):
    n_in = len(hops)
    a_refs, b_refs = refs[:n_in], refs[n_in:n_in + 2]
    out_ref, a_all, b_all = refs[-3:]
    z, yl, yh, c = pos[0] // 16, lax.rem(pos[0] // 4, 4), lax.rem(pos[0] // 2, 2), lax.rem(pos[0], 2)

    @pl.when(pl.program_id(0) == 0)
    def _():
        at = 0
        for ref in a_refs:
            rows = ref.shape[0] * 128
            a_all[pl.ds(at, rows), :] = ref[...].reshape(rows, 1024)
            at += rows

    for tile in range(2):
        for side in range(2):
            inner = lax.rem(yh + tile, 2) * 2 + lax.rem(c + side, 2)
            b_all[:, inner] = b_refs[side][:, tile * TILE:(tile + 1) * TILE]
    width = out_ref.shape[-1]
    res = jnp.dot(a_all[...], b_all[...].reshape(1024, width), preferred_element_type=jnp.float32)
    res = res.astype(out_ref.dtype)
    at = 0
    for ref, hop in zip(a_refs, hops):
        for j in range(ref.shape[0]):
            step = jnp.where(c == 0, 6, 2) if hop == 2 and ref.shape[0] == 2 else hop
            block = lax.rem(z + step + 4 * j, 8)
            column = lax.rem(block, 4) if out_ref.shape[1] > 1 else 0
            for k in range(4):
                row = pl.multiple_of(jnp.bitwise_xor(yl, k) * 32, 32)
                out_ref[block // 4, column, pl.ds(row, 32), :] = res[at:at + 32]
                at += 32


def matmul(hops, pos, a_pieces, b_pieces, base=None, width=512):
    if base is None:
        out_spec = pl.BlockSpec((2, 4, 128, width), lambda s, pos: (0, 0, 0, s))
    else:
        out_spec = pl.BlockSpec((2, 1, 128, width), lambda s, pos: (0, lax.rem(pos[0] // 16 + hops[0], 4), 0, s))
    rows = sum(p.shape[0] for p in a_pieces) * 128
    grid_spec = pltpu.PrefetchScalarGridSpec(
        num_scalar_prefetch=1,
        grid=(2048 // width,),
        in_specs=[pl.BlockSpec(p.shape, lambda s, pos: (0, 0, 0)) for p in a_pieces]
        + [pl.BlockSpec((4, 128, width), lambda s, pos: (0, 0, s))] * 2
        + ([] if base is None else [pl.BlockSpec(memory_space=pl.ANY)]),
        out_specs=out_spec,
        scratch_shapes=[pltpu.VMEM((rows, 1024), jnp.bfloat16), pltpu.VMEM((4, 4, 64, width), jnp.bfloat16)],
    )
    more = () if base is None else (base,)
    return pl.pallas_call(
        lambda *refs: matmul_kernel(hops, *refs),
        grid_spec=grid_spec,
        out_shape=jax.ShapeDtypeStruct((2, 4, 128, 2048), jnp.bfloat16),
        input_output_aliases={} if base is None else {1 + len(a_pieces) + 2: 0},
        name="ladder_matmul" if base is None else "ladder_last",
    )(pos, *a_pieces, *b_pieces, *more)


def on_device(amplitudes, integrals, amp_mask, integral_mask):
    virt = (lax.axis_index("zh") * 4 + lax.axis_index("zl")) * 4 + lax.axis_index("yl")
    pos = (virt * 4 + lax.axis_index("yh") * 2 + lax.axis_index("c")).reshape(1)
    own_a, own_b = prep(pos, amp_mask, integral_mask, amplitudes, integrals)
    far_b = shift(own_b, "yh", 2, 1)
    a_two = jnp.concatenate([own_a[None, None], shift_z(own_a, 4)[None, None]])
    a0 = jnp.concatenate([a_two] + [swap_y(a_two, k) for k in (1, 2, 3)], axis=1)
    a0 = a0.reshape(2, 128, 1024)
    here = all_x(jnp.broadcast_to(jnp.concatenate([own_b, far_b])[None], (4, 128, 2048)))
    there = shift(here, "c", 2, 1)
    b_pieces = [here, there]
    a1, a3 = shift_z(a0, -1), shift_z(a0, 1)
    f1, f3 = shift_z(a1[:1], -1), shift_z(a3[:1], 1)
    out = matmul((0, 1, 7, 2, 6), pos, [a0, a1, a3, f1, f3], b_pieces)
    return out.reshape(1024, 2048)


def solution(mesh):
    fine = Mesh(mesh.devices.reshape(4, 2, 2, 2, 4, 4), AXES)
    pair, virt = AXES[:3], AXES[3:]
    in_specs = (P(AXES, None), P(pair, virt), P(pair, None), P(pair, virt))
    return jax.shard_map(on_device, mesh=fine, in_specs=in_specs, out_specs=P(pair, virt), check_vma=False)
```

```python
import jax
import jax.numpy as jnp
from jax import lax
from jax.experimental import pallas as pl
from jax.experimental.pallas import tpu as pltpu
from jax.sharding import Mesh, PartitionSpec as P


TILE = 64
AXES = ("x", "yh", "c", "zh", "zl", "yl")


def prep_kernel(pos, am_ref, im_ref, a_ref, b_ref, own_a_ref, own_b_ref):
    tile_row = pos[0] // 8
    lane = lax.broadcasted_iota(jnp.int32, (8, 128), 1)

    def spread(low, high):
        both = jnp.where(lane < TILE, low, high)[:1]
        return both.astype(jnp.float32).astype(jnp.bfloat16)

    for g in range(16):
        span = pl.ds(g * 128, 128)
        own_b_ref[:, span] = b_ref[:, span] * spread(im_ref[0, 2 * g], im_ref[0, 2 * g + 1])
    for g in range(8):
        span = pl.ds(g * 128, 128)
        own_a_ref[:, span] = a_ref[:, span] * spread(am_ref[tile_row, 2 * g], am_ref[tile_row, 2 * g + 1])


def prep(pos, amp_mask, integral_mask, amplitudes, integrals):
    smem, vmem = pl.BlockSpec(memory_space=pltpu.SMEM), pl.BlockSpec(memory_space=pltpu.VMEM)
    shapes = ((32, 1024), (64, 2048))
    return pl.pallas_call(
        prep_kernel,
        in_specs=[smem, smem, smem, vmem, vmem],
        out_specs=[vmem] * 2,
        out_shape=[jax.ShapeDtypeStruct(s, jnp.bfloat16) for s in shapes],
        name="prep",
    )(pos, amp_mask, integral_mask, amplitudes, integrals)


def shift_z(value, by):
    return lax.ppermute(value, ("zh", "zl"), [(z, (z + by) % 8) for z in range(8)])


def shift(value, axis, size, by):
    return lax.ppermute(value, axis, [(i, (i + by) % size) for i in range(size)])


def swap_y(value, by):
    return lax.ppermute(value, "yl", [(y, y ^ by) for y in range(4)])


def all_x(fan):
    return lax.all_to_all(fan, "x", 0, 0)


def matmul_kernel(hops, width, pos, *refs):
    n_in = len(hops)
    a_refs, b_refs = refs[:n_in], refs[n_in:n_in + 2]
    out_ref, a_all, b_all, a_sems, b_sems = refs[-5:]
    step = pl.program_id(0)
    z, yl, yh, c = pos[0] // 16, lax.rem(pos[0] // 4, 4), lax.rem(pos[0] // 2, 2), lax.rem(pos[0], 2)

    def b_copies(block):
        columns = pl.ds(pl.multiple_of(block * width, width), width)
        return [
            pltpu.make_async_copy(
                b_refs[side].at[:, pl.ds(tile * TILE, TILE), columns],
                b_all.at[:, lax.rem(yh + tile, 2) * 2 + lax.rem(c + side, 2), :, columns],
                b_sems.at[block, tile * 2 + side],
            )
            for tile in range(2)
            for side in range(2)
        ]

    def a_copies():
        copies, at = [], 0
        for n, ref in enumerate(a_refs):
            copies.append(pltpu.make_async_copy(ref, a_all.at[pl.ds(at, ref.shape[0])], a_sems.at[n]))
            at += ref.shape[0]
        return copies

    @pl.when(step == 0)
    def _():
        for copy in b_copies(0) + a_copies():
            copy.start()
        for block in range(1, 2048 // width):
            for copy in b_copies(block):
                copy.start()
        for copy in a_copies():
            copy.wait()

    for copy in b_copies(step):
        copy.wait()
    columns = pl.ds(pl.multiple_of(step * width, width), width)
    a_value = a_all[...].reshape(1024, 1024)
    b_value = b_all[:, :, :, columns].reshape(1024, width)
    res = jnp.dot(a_value, b_value, preferred_element_type=jnp.float32).astype(out_ref.dtype)
    at = 0
    for ref, hop in zip(a_refs, hops):
        for j in range(ref.shape[0]):
            block = lax.rem(z + hop + 4 * j, 8)
            for k in range(4):
                row = pl.multiple_of(jnp.bitwise_xor(yl, k) * 32, 32)
                out_ref[block, pl.ds(row, 32), :] = res[at:at + 32]
                at += 32


def matmul(hops, pos, a_pieces, b_pieces, width=512):
    n_in = len(hops)
    any_spec = pl.BlockSpec(memory_space=pl.ANY)
    grid_spec = pltpu.PrefetchScalarGridSpec(
        num_scalar_prefetch=1,
        grid=(2048 // width,),
        in_specs=[any_spec] * (n_in + 2),
        out_specs=pl.BlockSpec((8, 128, width), lambda s, pos: (0, 0, s)),
        scratch_shapes=[
            pltpu.VMEM((8, 128, 1024), jnp.bfloat16),
            pltpu.VMEM((4, 4, 64, 2048), jnp.bfloat16),
            pltpu.SemaphoreType.DMA((n_in,)),
            pltpu.SemaphoreType.DMA((2048 // width, 4)),
        ],
    )
    return pl.pallas_call(
        lambda *refs: matmul_kernel(hops, width, *refs),
        grid_spec=grid_spec,
        out_shape=jax.ShapeDtypeStruct((8, 128, 2048), jnp.bfloat16),
        name="ladder_matmul",
    )(pos, *a_pieces, *b_pieces)


def on_device(amplitudes, integrals, amp_mask, integral_mask):
    virt = (lax.axis_index("zh") * 4 + lax.axis_index("zl")) * 4 + lax.axis_index("yl")
    pos = (virt * 4 + lax.axis_index("yh") * 2 + lax.axis_index("c")).reshape(1)
    own_a, own_b = prep(pos, amp_mask, integral_mask, amplitudes, integrals)
    far_b = shift(own_b, "yh", 2, 1)
    a_two = jnp.concatenate([own_a[None, None], shift_z(own_a, 4)[None, None]])
    a0 = jnp.concatenate([a_two] + [swap_y(a_two, k) for k in (1, 2, 3)], axis=1)
    a0 = a0.reshape(2, 128, 1024)
    here = all_x(jnp.broadcast_to(jnp.concatenate([own_b, far_b])[None], (4, 128, 2048)))
    there = shift(here, "c", 2, 1)
    b_pieces = [here, there]
    a1, a3 = shift_z(a0, -1), shift_z(a0, 1)
    f1, f3 = shift_z(a1[:1], -1), shift_z(a3[:1], 1)
    out = matmul((0, 1, 7, 2, 6), pos, [a0, a1, a3, f1, f3], b_pieces)
    return out.reshape(1024, 2048)


def solution(mesh):
    fine = Mesh(mesh.devices.reshape(4, 2, 2, 2, 4, 4), AXES)
    pair, virt = AXES[:3], AXES[3:]
    in_specs = (P(AXES, None), P(pair, virt), P(pair, None), P(pair, virt))
    return jax.shard_map(on_device, mesh=fine, in_specs=in_specs, out_specs=P(pair, virt), check_vma=False)
```
